32 devices in a mesh: row: 8 (over y, x, core), col: 4 (over z).
Axes of the slice: x: 2, y: 2, z: 4, core: 2. Of those that a mesh axis runs over, the one named last changes fastest.
Arguments:
- a_blocks: bfloat16 [3328, 128, 128], P(('row', 'col')), may hold values from -6 to 6
- a_coord: int32 [3328, 2], P(('row', 'col')), may hold values from 0 to 111, as said below
- b_blocks: bfloat16 [1664, 128, 128], P(('row', 'col')), may hold values from -0.099609375 to 0.099609375
- b_coord: int32 [1664, 2], P(('row', 'col')), may hold values from 0 to 55, as said below
- c_keep: int32 [112, 56], P('row', 'col'), may hold values 0 or 1
Outputs:
- c_window: bfloat16 [14336, 7168], P('row', 'col')
The draws below stay inside these ranges and needn't reach their ends.
Inputs may be any that keep to these rules, and one draw needn't show every extreme that they name: `a_coord`: every row names a distinct block of dense_a. A block (I, K) belongs to the device of grid row I // 14 and grid column (K // 8 - I // 14) mod 4; among the 104 rows of one device, at most 4 name blocks of the same device, and every device that is named at all is named exactly 4 times. `b_coord`: every row names a distinct block of dense_b. A block (K, J) belongs to the devices of grid column J // 14 and every grid row r with (r + J // 14) mod 4 = K // 8; among the 52 rows of one device, at most 4 name blocks of the same device, and every device that is named at all is named exactly 4 times.
All inputs are finite; a program needn't handle non-finite values. No bound on the sum of `c_keep` on one device may be relied on, other than what follows from the above.
Results may differ from the reference program's by a relative error of at most 0.001.
Values may be sent and summed in bfloat16 or wider, within the bound.
A program may use at most 192 MiB of HBM per device.

```python
import jax
import jax.numpy as jnp
from jax import lax

BS = 128
RB = 14
CB = 14
KB = 8
LIVE = 104
STEPS = 4
CAP = 4
MBT = 112
KBT = 32
NBT = 56
BSLOT = 52
N_ROW = 8
N_COL = 4
DEVICES = 32


def shuffle_one(subkey, positions):
    return jax.random.permutation(subkey, positions)


def spread(key, panels, positions):
    groups = LIVE // CAP
    per_source = panels * groups // DEVICES
    sources = jax.random.permutation(jax.random.fold_in(key, 1), DEVICES).astype(jnp.int32)
    subkeys = jax.random.split(jax.random.fold_in(key, 2), panels)
    orders = jax.vmap(lambda subkey: shuffle_one(subkey, positions))(subkeys).astype(jnp.int32)
    rounds = jnp.arange(per_source, dtype=jnp.int32)
    global_group = rounds[None, :] * DEVICES + sources[:, None]
    panel_id = global_group // groups
    offset = (global_group % groups)[:, :, None] * CAP + jnp.arange(CAP, dtype=jnp.int32)[None, None, :]
    where_in = orders[panel_id[:, :, None], offset]
    panel_all = jnp.broadcast_to(panel_id[:, :, None], where_in.shape)
    return (panel_all.reshape(-1), where_in.reshape(-1))


def draw_a_coord(key, part):
    panel_id, where_in = spread(jax.random.fold_in(key, 101), DEVICES, RB * KB)
    grid_row = panel_id // N_COL
    grid_col = panel_id % N_COL
    k_part = (grid_row + grid_col) % N_COL
    block_row = grid_row * RB + where_in // KB
    block_col = k_part * KB + where_in % KB
    return jnp.stack([block_row, block_col], axis=1).astype(jnp.int32)


def draw_b_coord(key, part):
    panel_id, where_in = spread(jax.random.fold_in(key, 202), N_COL * N_COL, KB * CB)
    k_part = panel_id // N_COL
    grid_col = panel_id % N_COL
    block_row = k_part * KB + where_in // CB
    block_col = grid_col * CB + where_in % CB
    return jnp.stack([block_row, block_col], axis=1).astype(jnp.int32)


def place_ends(drawn, stream_key, smallest, top_value):
    longest = drawn.shape.index(max(drawn.shape))
    spots = []
    for shift in (0, 1):
        where = [jax.random.randint(jax.random.fold_in(stream_key, axis), (), 0, length) for axis, length in enumerate(drawn.shape)]
        where[longest] = (where[longest] + shift) % drawn.shape[longest]
        spots.append(tuple(where))
    return drawn.at[spots[0]].set(smallest).at[spots[1]].set(top_value)


def block_levels(rng, dims, cuts, low, high):
    loudness, own = 1.0, jax.random.fold_in(rng, 6)
    for position, shards_of in cuts:
        draws = jnp.exp(jax.random.uniform(jax.random.fold_in(own, position), (shards_of,), jnp.float32, low / len(cuts), high / len(cuts)))
        loudness = loudness * jnp.repeat(draws, dims[position] // shards_of).reshape([-1 if axis == position else 1 for axis in range(len(dims))])
    return loudness


def noise(own_key, dims, deviation, reach, pieces=(), kind=jnp.bfloat16):
    array = jax.random.normal(own_key, dims, jnp.float32) * deviation
    if len(pieces) > 0:
        array = block_levels(own_key, dims, pieces, -0.22, 0.18) * array
    return jnp.clip(array, min=-reach, max=reach).astype(kind)


def setup_inputs(seed: int = 0) -> dict:
    keys = jax.random.split(jax.random.key(seed), 6)
    a_blocks = noise(keys[0], (DEVICES * LIVE, BS, BS), 1.0, 6.0, ((0, 32),))
    a_coord = draw_a_coord(jax.random.fold_in(keys[5], 71), 0)
    b_blocks = noise(keys[2], (DEVICES * BSLOT, BS, BS), 0.016, 0.099609375, ((0, 32),))
    b_coord = draw_b_coord(jax.random.fold_in(keys[5], 71), 0)
    c_keep = place_ends((jax.random.randint(keys[4], (MBT, NBT), 0, 4) < 3).astype(jnp.int32), jax.random.fold_in(keys[4], 1), 0, 1)
    return {"a_blocks": a_blocks, "a_coord": a_coord, "b_blocks": b_blocks, "b_coord": b_coord, "c_keep": c_keep}


def reference(a_blocks, a_coord, b_blocks, b_coord, c_keep):
    edge_size = a_blocks.shape[1]
    dense_a = jnp.zeros((MBT, KBT, edge_size, edge_size), jnp.bfloat16).at[a_coord[:, 0], a_coord[:, 1]].set(a_blocks)
    dense_b = jnp.zeros((KBT, NBT, edge_size, edge_size), jnp.bfloat16).at[b_coord[:, 0], b_coord[:, 1]].set(b_blocks)
    parts_b = dense_b.reshape(N_COL, KB, N_COL, CB, edge_size, edge_size)
    columns = jnp.arange(N_COL, dtype=jnp.int32)

    def one_row(row_index):
        a_rows = lax.dynamic_slice_in_dim(dense_a, row_index * RB, RB, 0).reshape(RB, N_COL, KB, edge_size, edge_size)
        summed = jnp.zeros((RB, N_COL, CB, edge_size, edge_size), jnp.float32)
        for step_index in range(STEPS):
            k_part = (row_index + columns + step_index) % N_COL
            a_panel = a_rows[:, k_part].astype(jnp.float32)
            b_panel = parts_b[k_part, :, columns].astype(jnp.float32)
            summed = summed + jnp.einsum("ucwxy,cwvyz->ucvxz", a_panel, b_panel)
        filter_mask = lax.dynamic_slice_in_dim(c_keep, row_index * RB, RB, 0).reshape(RB, N_COL, CB).astype(jnp.float32)
        summed = summed * filter_mask[:, :, :, None, None]
        return summed.transpose(0, 3, 1, 2, 4).reshape(RB * edge_size, NBT * edge_size).astype(jnp.bfloat16)

    stacked = lax.map(one_row, jnp.arange(N_ROW, dtype=jnp.int32))
    return stacked.reshape(MBT * edge_size, NBT * edge_size)
```

```python
import functools

import jax
import jax.numpy as jnp
from jax import lax
from jax.experimental import pallas as pl
from jax.experimental.pallas import tpu as pltpu
from jax.sharding import PartitionSpec as P

KB = 8
STEPS = 4
MESH = pl.DeviceIdType.MESH


def from_behind(value, axis, steps):
    count = lax.axis_size(axis)
    pairs = [(source, (source + steps) % count) for source in range(count)]
    return lax.ppermute(value, axis, pairs)


def slot_targets(owners, devices, capacity):
    matches = (owners[:, None] == jnp.arange(devices, dtype=jnp.int32)[None, :]).astype(jnp.int32)
    order_rank = jnp.sum((jnp.cumsum(matches, axis=0) - 1) * matches, axis=1)
    return owners * capacity + order_rank


def as_slots(values, slot_count, trailing):
    return values.reshape((slot_count,) + trailing)


def stepwise(a_blocks, a_coord, b_blocks, b_coord, c_keep):
    n_rows = lax.axis_size("row")
    n_cols = lax.axis_size("col")
    devices = n_rows * n_cols
    copies = n_rows // n_cols
    capacity = max(2, 128 // devices)
    slot_count = devices * capacity
    edge_size = a_blocks.shape[1]
    block_rows, block_cols = c_keep.shape
    a_grid_row = a_coord[:, 0] // block_rows
    a_part = a_coord[:, 1] // KB
    a_owner = a_grid_row * n_cols + (a_part - a_grid_row) % n_cols
    a_target = slot_targets(a_owner, devices, capacity)
    b_part = b_coord[:, 0] // KB
    b_grid_col = b_coord[:, 1] // block_cols
    b_first = (b_part - b_grid_col) % n_cols
    copy_rows = b_first[:, None] + n_cols * jnp.arange(copies, dtype=jnp.int32)[None, :]
    b_owner = (copy_rows * n_cols + b_grid_col[:, None]).reshape(-1)
    b_target = slot_targets(b_owner, devices, capacity)
    b_source = jnp.repeat(jnp.arange(b_blocks.shape[0], dtype=jnp.int32), copies)
    a_send = jnp.zeros((slot_count, edge_size, edge_size), jnp.bfloat16).at[a_target].set(a_blocks)
    a_where = jnp.full((slot_count, 2), -1, jnp.int32).at[a_target].set(a_coord)
    b_send = (
        jnp.zeros((slot_count, edge_size, edge_size), jnp.bfloat16)
        .at[b_target]
        .set(b_blocks[b_source])
    )
    b_where = jnp.full((slot_count, 2), -1, jnp.int32).at[b_target].set(b_coord[b_source])

    def exchange(values, trailing):
        shaped = values.reshape((devices, capacity) + values.shape[1:])
        got = lax.all_to_all(shaped, ("row", "col"), split_axis=0, concat_axis=0, tiled=True)
        return as_slots(got, slot_count, trailing)

    a_recv = exchange(a_send, (edge_size, edge_size))
    b_recv = exchange(b_send, (edge_size, edge_size))
    a_from = exchange(a_where, (2,))
    b_from = exchange(b_where, (2,))
    a_slot_row = jnp.where(a_from[:, 0] >= 0, a_from[:, 0] % block_rows, block_rows)
    a_panel = (
        jnp.zeros((block_rows, edge_size, KB, edge_size), jnp.bfloat16)
        .at[a_slot_row, :, a_from[:, 1] % KB, :]
        .set(a_recv, mode="drop")
    )
    a_matrix = a_panel.reshape(block_rows * edge_size, KB * edge_size)
    b_slot_row = jnp.where(b_from[:, 0] >= 0, b_from[:, 0] % KB, KB)
    b_panel = (
        jnp.zeros((KB, edge_size, block_cols, edge_size), jnp.bfloat16)
        .at[b_slot_row, :, b_from[:, 1] % block_cols, :]
        .set(b_recv, mode="drop")
    )
    b_matrix = b_panel.reshape(KB * edge_size, block_cols * edge_size)
    summed = jnp.zeros((block_rows * edge_size, block_cols * edge_size), jnp.float32)
    for step_index in range(STEPS):
        summed = summed + jnp.dot(a_matrix, b_matrix, preferred_element_type=jnp.float32)
        if step_index + 1 < STEPS:
            a_matrix = from_behind(a_matrix, "col", -1)
            b_matrix = from_behind(b_matrix, "row", -1)
    masked = (
        summed.reshape(block_rows, edge_size, block_cols, edge_size)
        * c_keep.astype(jnp.float32)[:, None, :, None]
    )
    return masked.reshape(block_rows * edge_size, block_cols * edge_size).astype(jnp.bfloat16)


def fused_kernel(
    n_rows, n_cols, cap, rb, cb, bs,
    a_index, b_index, a_send, b_send, keep, out,
    a_parts, b_parts, a_dense, b_dense, acc, stage,
    ax_send, ax_recv, bz_send, bz_recv, bx_send, bx_recv, az_send, az_recv, own_sem, out_sem,
):
    r = lax.axis_index("row")
    z = lax.axis_index("col")
    plane = n_rows * cap
    line = n_cols * cap
    zero_slot = n_rows * n_cols * cap

    barrier = pltpu.get_barrier_semaphore()
    for d in range(1, n_rows):
        pl.semaphore_signal(barrier, inc=1, device_id=(lax.rem(r + d, n_rows), z), device_id_type=MESH)
    for d in range(1, n_cols):
        pl.semaphore_signal(barrier, inc=1, device_id=(r, lax.rem(z + d, n_cols)), device_id_type=MESH)
    pl.semaphore_wait(barrier, n_rows + n_cols - 2)

    def ax(p, d):
        to = lax.rem(r + d, n_rows)
        return pltpu.make_async_remote_copy(
            src_ref=a_send.at[p, to],
            dst_ref=a_parts[p].at[pl.ds(z * plane + r * cap, cap)],
            send_sem=ax_send.at[p, d - 1],
            recv_sem=ax_recv.at[p, d - 1],
            device_id=(to, z),
            device_id_type=MESH,
        )

    def ax_own(p):
        return pltpu.make_async_copy(
            a_send.at[p, r], a_parts[p].at[pl.ds(z * plane + r * cap, cap)], own_sem.at[0, p]
        )

    def bz(p, d):
        to = lax.rem(z + d, n_cols)
        return pltpu.make_async_remote_copy(
            src_ref=b_send.at[p, to],
            dst_ref=b_parts[p].at[pl.ds(r * line + z * cap, cap)],
            send_sem=bz_send.at[p, d - 1],
            recv_sem=bz_recv.at[p, d - 1],
            device_id=(r, to),
            device_id_type=MESH,
        )

    def bz_own(p):
        return pltpu.make_async_copy(
            b_send.at[p, z], b_parts[p].at[pl.ds(r * line + z * cap, cap)], own_sem.at[1, p]
        )

    def bx(p, d):
        section = b_parts[p].at[pl.ds(r * line, line)]
        return pltpu.make_async_remote_copy(
            src_ref=section,
            dst_ref=section,
            send_sem=bx_send.at[p, d - 1],
            recv_sem=bx_recv.at[p, d - 1],
            device_id=(lax.rem(r + d, n_rows), z),
            device_id_type=MESH,
        )

    def az(p, hop, way):
        origin = z - hop * way
        section = a_parts[p].at[pl.ds(origin * plane, plane)]
        return pltpu.make_async_remote_copy(
            src_ref=section,
            dst_ref=section,
            send_sem=az_send.at[p, hop, (way + 1) // 2],
            recv_sem=az_recv.at[p, hop, (way + 1) // 2],
            device_id=(r, z + way),
            device_id_type=MESH,
        )

    def arrived(p, hop, way):
        section = a_parts[p].at[pl.ds((z - hop * way) * plane, plane)]
        return pltpu.make_async_remote_copy(
            src_ref=section,
            dst_ref=section,
            send_sem=az_send.at[p, hop - 1, (way + 1) // 2],
            recv_sem=az_recv.at[p, hop - 1, (way + 1) // 2],
            device_id=(r, z - way),
            device_id_type=MESH,
        )

    def can_send(hop, way):
        if way == 1:
            return jnp.logical_and(z >= hop, z < n_cols - 1)
        return jnp.logical_and(z + hop < n_cols, z > 0)

    def can_receive(hop, way):
        return z >= hop if way == 1 else z + hop < n_cols

    def open_part(p):
        for d in range(1, n_rows):
            ax(p, d).wait_recv()
        ax_own(p).wait()
        for way in (1, -1):
            @pl.when(can_send(0, way))
            def _():
                az(p, 0, way).start()
        for d in range(1, n_cols):
            bz(p, d).wait_recv()
        bz_own(p).wait()
        for d in range(1, n_rows):
            bx(p, d).start()

    def relay(p):
        for hop in range(1, n_cols):
            for way in (1, -1):
                @pl.when(can_receive(hop, way))
                def _():
                    arrived(p, hop, way).wait_recv()
                if hop < n_cols - 1:
                    @pl.when(can_send(hop, way))
                    def _():
                        az(p, hop, way).start()

    def multiply(p):
        for d in range(1, n_rows):
            bx(p, d).wait_recv()

        def place_a(i, carry):
            rows = pl.ds(pl.multiple_of(i * bs, bs), bs)
            for k in range(KB):
                a_dense[rows, k * bs:(k + 1) * bs] = a_parts[p][a_index[p, i * KB + k]]
            return carry

        lax.fori_loop(0, rb, place_a, 0)

        def place_b(k, carry):
            rows = pl.ds(pl.multiple_of(k * bs, bs), bs)
            for j in range(cb):
                b_dense[rows, j * bs:(j + 1) * bs] = b_parts[p][b_index[p, k * cb + j]]
            return carry

        lax.fori_loop(0, KB, place_b, 0)

        wide = 2 * bs
        tall = rb * bs // 2

        def tile(t, carry):
            rows = pl.ds(pl.multiple_of((t % 2) * tall, tall), tall)
            cols = pl.ds(pl.multiple_of((t // 2) * wide, wide), wide)
            term = jnp.dot(a_dense[rows, :], b_dense[:, cols], preferred_element_type=jnp.float32)
            acc[rows, cols] = term if p == 0 else acc[rows, cols] + term
            return carry

        lax.fori_loop(0, 2 * (cb * bs // wide), tile, 0)

    for p in range(n_cols):
        for d in range(1, n_rows):
            ax(p, d).start()
        ax_own(p).start()
        for d in range(1, n_cols):
            bz(p, d).start()
        bz_own(p).start()
    for p in range(n_cols):
        a_parts[p][zero_slot] = jnp.zeros((bs, bs), jnp.bfloat16)
        b_parts[p][zero_slot] = jnp.zeros((bs, bs), jnp.bfloat16)

    open_part(0)
    for p in range(n_cols):
        if p + 1 < n_cols:
            open_part(p + 1)
        relay(p)
        multiply(p)

    def finish(i):
        return pltpu.make_async_copy(
            stage.at[i * bs:(i + 1) * bs], out.at[i * bs:(i + 1) * bs], out_sem.at[i]
        )

    for i in range(rb):
        rows = slice(i * bs, (i + 1) * bs)
        stage[rows, :] = (acc[rows, :] * keep[i:i + 1, :]).astype(jnp.bfloat16)
        finish(i).start()
    for p in range(n_cols):
        for d in range(1, n_rows):
            ax(p, d).wait_send()
            bx(p, d).wait_send()
        for d in range(1, n_cols):
            bz(p, d).wait_send()
        for hop in range(n_cols - 1):
            for way in (1, -1):
                @pl.when(can_send(hop, way))
                def _():
                    az(p, hop, way).wait_send()
    for i in range(rb):
        finish(i).wait()


def slot_sources(owner, count, cap):
    same = owner[:, None] == owner[None, :]
    total = owner.shape[0]
    earlier = jnp.arange(total)[None, :] < jnp.arange(total)[:, None]
    rank = jnp.sum((same & earlier).astype(jnp.int32), axis=1)
    target = owner * cap + rank
    hit = target[:, None] == jnp.arange(count * cap, dtype=jnp.int32)[None, :]
    order = jnp.arange(total, dtype=jnp.int32)[:, None]
    return jnp.max(jnp.where(hit, order, -1), axis=0), hit


def gathered(a_blocks, a_coord, b_blocks, b_coord, c_keep):
    n_rows = lax.axis_size("row")
    n_cols = lax.axis_size("col")
    devices = n_rows * n_cols
    cap = max(2, 128 // devices)
    bs = a_blocks.shape[1]
    rb, cb = c_keep.shape
    a_owner = (a_coord[:, 1] // KB) * n_rows + a_coord[:, 0] // rb
    b_owner = (b_coord[:, 0] // KB) * n_cols + b_coord[:, 1] // cb
    a_source, a_hit = slot_sources(a_owner, devices, cap)
    b_source, b_hit = slot_sources(b_owner, n_cols * n_cols, cap)
    a_place = (a_coord[:, 0] % rb) * KB + a_coord[:, 1] % KB
    b_place = (b_coord[:, 0] % KB) * cb + b_coord[:, 1] % cb
    a_slot = jnp.max(jnp.where(a_hit, a_place[:, None], -1), axis=0)
    b_slot = jnp.max(jnp.where(b_hit, b_place[:, None], -1), axis=0)
    a_send = jnp.take(a_blocks, jnp.maximum(a_source, 0), axis=0, mode="clip")
    b_send = jnp.take(b_blocks, jnp.maximum(b_source, 0), axis=0, mode="clip")
    a_send = a_send.reshape(n_cols, n_rows, cap, bs, bs)
    b_send = b_send.reshape(n_cols, n_cols, cap, bs, bs)

    slots = lax.all_gather(jnp.concatenate([a_slot, b_slot]), ("row", "col"))
    r = lax.axis_index("row")
    z = lax.axis_index("col")
    a_all = slots[:, : devices * cap].reshape(n_rows, n_cols, n_cols, n_rows, cap)
    a_mine = lax.dynamic_index_in_dim(a_all, r, 3, keepdims=False)
    a_mine = a_mine.transpose(2, 1, 0, 3).reshape(n_cols, devices * cap)
    b_all = slots[:, devices * cap:].reshape(n_rows, n_cols, n_cols, n_cols, cap)
    b_mine = lax.dynamic_index_in_dim(b_all, z, 3, keepdims=False)
    b_mine = b_mine.transpose(2, 0, 1, 3).reshape(n_cols, devices * cap)

    def invert(mine, places):
        hit = mine[:, :, None] == jnp.arange(places, dtype=jnp.int32)[None, None, :]
        order = jnp.arange(devices * cap, dtype=jnp.int32)[None, :, None]
        return jnp.min(jnp.where(hit, order, devices * cap), axis=1)

    keep = jnp.repeat(c_keep.astype(jnp.float32), bs, axis=1)
    held = devices * cap + 1
    part = pltpu.VMEM((held, bs, bs), jnp.bfloat16)
    dma = pltpu.SemaphoreType.DMA
    return pl.pallas_call(
        functools.partial(fused_kernel, n_rows, n_cols, cap, rb, cb, bs),
        out_shape=jax.ShapeDtypeStruct((rb * bs, cb * bs), jnp.bfloat16),
        in_specs=[
            pl.BlockSpec(memory_space=pltpu.SMEM),
            pl.BlockSpec(memory_space=pltpu.SMEM),
            pl.BlockSpec(memory_space=pl.ANY),
            pl.BlockSpec(memory_space=pl.ANY),
            pl.BlockSpec(memory_space=pltpu.VMEM),
        ],
        out_specs=pl.BlockSpec(memory_space=pl.ANY),
        scratch_shapes=[
            [part] * n_cols,
            [part] * n_cols,
            pltpu.VMEM((rb * bs, KB * bs), jnp.bfloat16),
            pltpu.VMEM((KB * bs, cb * bs), jnp.bfloat16),
            pltpu.VMEM((rb * bs, cb * bs), jnp.float32),
            pltpu.VMEM((rb * bs, cb * bs), jnp.bfloat16),
            dma((n_cols, n_rows - 1)),
            dma((n_cols, n_rows - 1)),
            dma((n_cols, n_cols - 1)),
            dma((n_cols, n_cols - 1)),
            dma((n_cols, n_rows - 1)),
            dma((n_cols, n_rows - 1)),
            dma((n_cols, n_cols - 1, 2)),
            dma((n_cols, n_cols - 1, 2)),
            dma((2, n_cols)),
            dma((rb,)),
        ],
        compiler_params=pltpu.CompilerParams(
            collective_id=0, has_side_effects=True, vmem_limit_bytes=60 * 2**20
        ),
    )(invert(a_mine, rb * KB), invert(b_mine, KB * cb), a_send, b_send, keep)


def solution(mesh):
    whole_window = mesh.shape["col"] == STEPS
    return jax.shard_map(
        gathered if whole_window else stepwise,
        mesh=mesh,
        in_specs=(
            P(("row", "col"), None, None),
            P(("row", "col"), None),
            P(("row", "col"), None, None),
            P(("row", "col"), None),
            P("row", "col"),
        ),
        out_specs=P("row", "col"),
        check_vma=False,
    )
```

```python
import functools

import jax
import jax.numpy as jnp
from jax import lax
from jax.experimental import pallas as pl
from jax.experimental.pallas import tpu as pltpu
from jax.sharding import PartitionSpec as P

KB = 8
STEPS = 4
MESH = pl.DeviceIdType.MESH


def from_behind(value, axis, steps):
    count = lax.axis_size(axis)
    pairs = [(source, (source + steps) % count) for source in range(count)]
    return lax.ppermute(value, axis, pairs)


def slot_targets(owners, devices, capacity):
    matches = (owners[:, None] == jnp.arange(devices, dtype=jnp.int32)[None, :]).astype(jnp.int32)
    order_rank = jnp.sum((jnp.cumsum(matches, axis=0) - 1) * matches, axis=1)
    return owners * capacity + order_rank


def as_slots(values, slot_count, trailing):
    return values.reshape((slot_count,) + trailing)


def stepwise(a_blocks, a_coord, b_blocks, b_coord, c_keep):
    n_rows = lax.axis_size("row")
    n_cols = lax.axis_size("col")
    devices = n_rows * n_cols
    copies = n_rows // n_cols
    capacity = max(2, 128 // devices)
    slot_count = devices * capacity
    edge_size = a_blocks.shape[1]
    block_rows, block_cols = c_keep.shape
    a_grid_row = a_coord[:, 0] // block_rows
    a_part = a_coord[:, 1] // KB
    a_owner = a_grid_row * n_cols + (a_part - a_grid_row) % n_cols
    a_target = slot_targets(a_owner, devices, capacity)
    b_part = b_coord[:, 0] // KB
    b_grid_col = b_coord[:, 1] // block_cols
    b_first = (b_part - b_grid_col) % n_cols
    copy_rows = b_first[:, None] + n_cols * jnp.arange(copies, dtype=jnp.int32)[None, :]
    b_owner = (copy_rows * n_cols + b_grid_col[:, None]).reshape(-1)
    b_target = slot_targets(b_owner, devices, capacity)
    b_source = jnp.repeat(jnp.arange(b_blocks.shape[0], dtype=jnp.int32), copies)
    a_send = jnp.zeros((slot_count, edge_size, edge_size), jnp.bfloat16).at[a_target].set(a_blocks)
    a_where = jnp.full((slot_count, 2), -1, jnp.int32).at[a_target].set(a_coord)
    b_send = (
        jnp.zeros((slot_count, edge_size, edge_size), jnp.bfloat16)
        .at[b_target]
        .set(b_blocks[b_source])
    )
    b_where = jnp.full((slot_count, 2), -1, jnp.int32).at[b_target].set(b_coord[b_source])

    def exchange(values, trailing):
        shaped = values.reshape((devices, capacity) + values.shape[1:])
        got = lax.all_to_all(shaped, ("row", "col"), split_axis=0, concat_axis=0, tiled=True)
        return as_slots(got, slot_count, trailing)

    a_recv = exchange(a_send, (edge_size, edge_size))
    b_recv = exchange(b_send, (edge_size, edge_size))
    a_from = exchange(a_where, (2,))
    b_from = exchange(b_where, (2,))
    a_slot_row = jnp.where(a_from[:, 0] >= 0, a_from[:, 0] % block_rows, block_rows)
    a_panel = (
        jnp.zeros((block_rows, edge_size, KB, edge_size), jnp.bfloat16)
        .at[a_slot_row, :, a_from[:, 1] % KB, :]
        .set(a_recv, mode="drop")
    )
    a_matrix = a_panel.reshape(block_rows * edge_size, KB * edge_size)
    b_slot_row = jnp.where(b_from[:, 0] >= 0, b_from[:, 0] % KB, KB)
    b_panel = (
        jnp.zeros((KB, edge_size, block_cols, edge_size), jnp.bfloat16)
        .at[b_slot_row, :, b_from[:, 1] % block_cols, :]
        .set(b_recv, mode="drop")
    )
    b_matrix = b_panel.reshape(KB * edge_size, block_cols * edge_size)
    summed = jnp.zeros((block_rows * edge_size, block_cols * edge_size), jnp.float32)
    for step_index in range(STEPS):
        summed = summed + jnp.dot(a_matrix, b_matrix, preferred_element_type=jnp.float32)
        if step_index + 1 < STEPS:
            a_matrix = from_behind(a_matrix, "col", -1)
            b_matrix = from_behind(b_matrix, "row", -1)
    masked = (
        summed.reshape(block_rows, edge_size, block_cols, edge_size)
        * c_keep.astype(jnp.float32)[:, None, :, None]
    )
    return masked.reshape(block_rows * edge_size, block_cols * edge_size).astype(jnp.bfloat16)


def fused_kernel(
    n_rows, n_cols, cap, rb, cb, bs,
    a_index, b_index, a_send, b_send, keep, out,
    a_parts, b_parts, a_dense, b_dense, acc, stage,
    ax_send, ax_recv, bz_send, bz_recv, bx_send, bx_recv, az_send, az_recv, own_sem, out_sem,
):
    r = lax.axis_index("row")
    z = lax.axis_index("col")
    plane = n_rows * cap
    line = n_cols * cap
    zero_slot = n_rows * n_cols * cap

    barrier = pltpu.get_barrier_semaphore()
    for d in range(1, n_rows):
        pl.semaphore_signal(barrier, inc=1, device_id=(lax.rem(r + d, n_rows), z), device_id_type=MESH)
    for d in range(1, n_cols):
        pl.semaphore_signal(barrier, inc=1, device_id=(r, lax.rem(z + d, n_cols)), device_id_type=MESH)
    pl.semaphore_wait(barrier, n_rows + n_cols - 2)

    def ax(p, d):
        to = lax.rem(r + d, n_rows)
        return pltpu.make_async_remote_copy(
            src_ref=a_send.at[p, to],
            dst_ref=a_parts[p].at[pl.ds(z * plane + r * cap, cap)],
            send_sem=ax_send.at[p, d - 1],
            recv_sem=ax_recv.at[p, d - 1],
            device_id=(to, z),
            device_id_type=MESH,
        )

    def ax_own(p):
        return pltpu.make_async_copy(
            a_send.at[p, r], a_parts[p].at[pl.ds(z * plane + r * cap, cap)], own_sem.at[0, p]
        )

    def bz(p, d):
        to = lax.rem(z + d, n_cols)
        return pltpu.make_async_remote_copy(
            src_ref=b_send.at[p, to],
            dst_ref=b_parts[p].at[pl.ds(r * line + z * cap, cap)],
            send_sem=bz_send.at[p, d - 1],
            recv_sem=bz_recv.at[p, d - 1],
            device_id=(r, to),
            device_id_type=MESH,
        )

    def bz_own(p):
        return pltpu.make_async_copy(
            b_send.at[p, z], b_parts[p].at[pl.ds(r * line + z * cap, cap)], own_sem.at[1, p]
        )

    def bx(p, d):
        section = b_parts[p].at[pl.ds(r * line, line)]
        return pltpu.make_async_remote_copy(
            src_ref=section,
            dst_ref=section,
            send_sem=bx_send.at[p, d - 1],
            recv_sem=bx_recv.at[p, d - 1],
            device_id=(lax.rem(r + d, n_rows), z),
            device_id_type=MESH,
        )

    def az(p, hop, way):
        origin = z - hop * way
        section = a_parts[p].at[pl.ds(origin * plane, plane)]
        return pltpu.make_async_remote_copy(
            src_ref=section,
            dst_ref=section,
            send_sem=az_send.at[p, hop, (way + 1) // 2],
            recv_sem=az_recv.at[p, hop, (way + 1) // 2],
            device_id=(r, z + way),
            device_id_type=MESH,
        )

    def arrived(p, hop, way):
        section = a_parts[p].at[pl.ds((z - hop * way) * plane, plane)]
        return pltpu.make_async_remote_copy(
            src_ref=section,
            dst_ref=section,
            send_sem=az_send.at[p, hop - 1, (way + 1) // 2],
            recv_sem=az_recv.at[p, hop - 1, (way + 1) // 2],
            device_id=(r, z - way),
            device_id_type=MESH,
        )

    def can_send(hop, way):
        if way == 1:
            return jnp.logical_and(z >= hop, z < n_cols - 1)
        return jnp.logical_and(z + hop < n_cols, z > 0)

    def can_receive(hop, way):
        return z >= hop if way == 1 else z + hop < n_cols

    def open_part(p):
        for d in range(1, n_rows):
            ax(p, d).wait_recv()
        ax_own(p).wait()
        for way in (1, -1):
            @pl.when(can_send(0, way))
            def _():
                az(p, 0, way).start()
        for d in range(1, n_cols):
            bz(p, d).wait_recv()
        bz_own(p).wait()
        for d in range(1, n_rows):
            bx(p, d).start()

    def relay(p):
        for hop in range(1, n_cols):
            for way in (1, -1):
                @pl.when(can_receive(hop, way))
                def _():
                    arrived(p, hop, way).wait_recv()
                if hop < n_cols - 1:
                    @pl.when(can_send(hop, way))
                    def _():
                        az(p, hop, way).start()

    def multiply(p):
        for d in range(1, n_rows):
            bx(p, d).wait_recv()

        def place_a(i, carry):
            rows = pl.ds(pl.multiple_of(i * bs, bs), bs)
            for k in range(KB):
                a_dense[rows, k * bs:(k + 1) * bs] = a_parts[p][a_index[p, i * KB + k]]
            return carry

        lax.fori_loop(0, rb, place_a, 0)

        def place_b(k, carry):
            rows = pl.ds(pl.multiple_of(k * bs, bs), bs)
            for j in range(cb):
                b_dense[rows, j * bs:(j + 1) * bs] = b_parts[p][b_index[p, k * cb + j]]
            return carry

        lax.fori_loop(0, KB, place_b, 0)

        wide = 2 * bs
        tall = rb * bs // 2

        def tile(t, carry):
            rows = pl.ds(pl.multiple_of((t % 2) * tall, tall), tall)
            cols = pl.ds(pl.multiple_of((t // 2) * wide, wide), wide)
            term = jnp.dot(a_dense[rows, :], b_dense[:, cols], preferred_element_type=jnp.float32)
            acc[rows, cols] = term if p == 0 else acc[rows, cols] + term
            return carry

        lax.fori_loop(0, 2 * (cb * bs // wide), tile, 0)

    for p in range(n_cols):
        for d in range(1, n_rows):
            ax(p, d).start()
        ax_own(p).start()
        for d in range(1, n_cols):
            bz(p, d).start()
        bz_own(p).start()
    for p in range(n_cols):
        a_parts[p][zero_slot] = jnp.zeros((bs, bs), jnp.bfloat16)
        b_parts[p][zero_slot] = jnp.zeros((bs, bs), jnp.bfloat16)

    open_part(0)
    for p in range(n_cols):
        if p + 1 < n_cols:
            open_part(p + 1)
        relay(p)
        multiply(p)

    def finish(i):
        return pltpu.make_async_copy(
            stage.at[i * bs:(i + 1) * bs], out.at[i * bs:(i + 1) * bs], out_sem.at[i]
        )

    for i in range(rb):
        rows = slice(i * bs, (i + 1) * bs)
        stage[rows, :] = (acc[rows, :] * keep[i:i + 1, :]).astype(jnp.bfloat16)
        finish(i).start()
    for p in range(n_cols):
        for d in range(1, n_rows):
            ax(p, d).wait_send()
            bx(p, d).wait_send()
        for d in range(1, n_cols):
            bz(p, d).wait_send()
        for hop in range(n_cols - 1):
            for way in (1, -1):
                @pl.when(can_send(hop, way))
                def _():
                    az(p, hop, way).wait_send()
    for i in range(rb):
        finish(i).wait()


def slot_sources(owner, count, cap):
    same = owner[:, None] == owner[None, :]
    total = owner.shape[0]
    earlier = jnp.arange(total)[None, :] < jnp.arange(total)[:, None]
    rank = jnp.sum((same & earlier).astype(jnp.int32), axis=1)
    target = owner * cap + rank
    hit = target[:, None] == jnp.arange(count * cap, dtype=jnp.int32)[None, :]
    order = jnp.arange(total, dtype=jnp.int32)[:, None]
    return jnp.max(jnp.where(hit, order, -1), axis=0), hit


def gathered(a_blocks, a_coord, b_blocks, b_coord, c_keep):
    n_rows = lax.axis_size("row")
    n_cols = lax.axis_size("col")
    devices = n_rows * n_cols
    cap = max(2, 128 // devices)
    bs = a_blocks.shape[1]
    rb, cb = c_keep.shape
    a_owner = (a_coord[:, 1] // KB) * n_rows + a_coord[:, 0] // rb
    b_owner = (b_coord[:, 0] // KB) * n_cols + b_coord[:, 1] // cb
    a_source, a_hit = slot_sources(a_owner, devices, cap)
    b_source, b_hit = slot_sources(b_owner, n_cols * n_cols, cap)
    a_place = (a_coord[:, 0] % rb) * KB + a_coord[:, 1] % KB
    b_place = (b_coord[:, 0] % KB) * cb + b_coord[:, 1] % cb
    a_slot = jnp.max(jnp.where(a_hit, a_place[:, None], -1), axis=0)
    b_slot = jnp.max(jnp.where(b_hit, b_place[:, None], -1), axis=0)
    a_send = jnp.take(a_blocks, jnp.maximum(a_source, 0), axis=0, mode="clip")
    b_send = jnp.take(b_blocks, jnp.maximum(b_source, 0), axis=0, mode="clip")
    a_send = a_send.reshape(n_cols, n_rows, cap, bs, bs)
    b_send = b_send.reshape(n_cols, n_cols, cap, bs, bs)

    a_to = a_slot.reshape(n_cols, n_rows, 1, cap).transpose(1, 2, 0, 3)
    b_to = b_slot.reshape(n_cols, 1, n_cols, cap).transpose(1, 2, 0, 3)
    shape = (n_rows, n_cols, n_cols, cap)
    both = jnp.stack([jnp.broadcast_to(a_to, shape), jnp.broadcast_to(b_to, shape)], axis=2)
    both = both.reshape(devices, 2 * n_cols * cap)
    slots = lax.all_to_all(both, ("row", "col"), split_axis=0, concat_axis=0, tiled=True)
    slots = slots.reshape(n_rows, n_cols, 2, n_cols, cap)
    a_mine = slots[:, :, 0].transpose(2, 1, 0, 3).reshape(n_cols, devices * cap)
    b_mine = slots[:, :, 1].transpose(2, 0, 1, 3).reshape(n_cols, devices * cap)

    def invert(mine, places):
        hit = mine[:, :, None] == jnp.arange(places, dtype=jnp.int32)[None, None, :]
        order = jnp.arange(devices * cap, dtype=jnp.int32)[None, :, None]
        return jnp.min(jnp.where(hit, order, devices * cap), axis=1)

    keep = jnp.repeat(c_keep.astype(jnp.float32), bs, axis=1)
    held = devices * cap + 1
    part = pltpu.VMEM((held, bs, bs), jnp.bfloat16)
    dma = pltpu.SemaphoreType.DMA
    return pl.pallas_call(
        functools.partial(fused_kernel, n_rows, n_cols, cap, rb, cb, bs),
        out_shape=jax.ShapeDtypeStruct((rb * bs, cb * bs), jnp.bfloat16),
        in_specs=[
            pl.BlockSpec(memory_space=pltpu.SMEM),
            pl.BlockSpec(memory_space=pltpu.SMEM),
            pl.BlockSpec(memory_space=pl.ANY),
            pl.BlockSpec(memory_space=pl.ANY),
            pl.BlockSpec(memory_space=pltpu.VMEM),
        ],
        out_specs=pl.BlockSpec(memory_space=pl.ANY),
        scratch_shapes=[
            [part] * n_cols,
            [part] * n_cols,
            pltpu.VMEM((rb * bs, KB * bs), jnp.bfloat16),
            pltpu.VMEM((KB * bs, cb * bs), jnp.bfloat16),
            pltpu.VMEM((rb * bs, cb * bs), jnp.float32),
            pltpu.VMEM((rb * bs, cb * bs), jnp.bfloat16),
            dma((n_cols, n_rows - 1)),
            dma((n_cols, n_rows - 1)),
            dma((n_cols, n_cols - 1)),
            dma((n_cols, n_cols - 1)),
            dma((n_cols, n_rows - 1)),
            dma((n_cols, n_rows - 1)),
            dma((n_cols, n_cols - 1, 2)),
            dma((n_cols, n_cols - 1, 2)),
            dma((2, n_cols)),
            dma((rb,)),
        ],
        compiler_params=pltpu.CompilerParams(
            collective_id=0, has_side_effects=True, vmem_limit_bytes=60 * 2**20
        ),
    )(invert(a_mine, rb * KB), invert(b_mine, KB * cb), a_send, b_send, keep)


def solution(mesh):
    whole_window = mesh.shape["col"] == STEPS
    return jax.shard_map(
        gathered if whole_window else stepwise,
        mesh=mesh,
        in_specs=(
            P(("row", "col"), None, None),
            P(("row", "col"), None),
            P(("row", "col"), None, None),
            P(("row", "col"), None),
            P("row", "col"),
        ),
        out_specs=P("row", "col"),
        check_vma=False,
    )
```

```python
import functools

import jax
import jax.numpy as jnp
from jax import lax
from jax.experimental import pallas as pl
from jax.experimental.pallas import tpu as pltpu
from jax.sharding import PartitionSpec as P

KB = 8
STEPS = 4
MESH = pl.DeviceIdType.MESH


def from_behind(value, axis, steps):
    count = lax.axis_size(axis)
    pairs = [(source, (source + steps) % count) for source in range(count)]
    return lax.ppermute(value, axis, pairs)


def slot_targets(owners, devices, capacity):
    matches = (owners[:, None] == jnp.arange(devices, dtype=jnp.int32)[None, :]).astype(jnp.int32)
    order_rank = jnp.sum((jnp.cumsum(matches, axis=0) - 1) * matches, axis=1)
    return owners * capacity + order_rank


def as_slots(values, slot_count, trailing):
    return values.reshape((slot_count,) + trailing)


def stepwise(a_blocks, a_coord, b_blocks, b_coord, c_keep):
    n_rows = lax.axis_size("row")
    n_cols = lax.axis_size("col")
    devices = n_rows * n_cols
    copies = n_rows // n_cols
    capacity = max(2, 128 // devices)
    slot_count = devices * capacity
    edge_size = a_blocks.shape[1]
    block_rows, block_cols = c_keep.shape
    a_grid_row = a_coord[:, 0] // block_rows
    a_part = a_coord[:, 1] // KB
    a_owner = a_grid_row * n_cols + (a_part - a_grid_row) % n_cols
    a_target = slot_targets(a_owner, devices, capacity)
    b_part = b_coord[:, 0] // KB
    b_grid_col = b_coord[:, 1] // block_cols
    b_first = (b_part - b_grid_col) % n_cols
    copy_rows = b_first[:, None] + n_cols * jnp.arange(copies, dtype=jnp.int32)[None, :]
    b_owner = (copy_rows * n_cols + b_grid_col[:, None]).reshape(-1)
    b_target = slot_targets(b_owner, devices, capacity)
    b_source = jnp.repeat(jnp.arange(b_blocks.shape[0], dtype=jnp.int32), copies)
    a_send = jnp.zeros((slot_count, edge_size, edge_size), jnp.bfloat16).at[a_target].set(a_blocks)
    a_where = jnp.full((slot_count, 2), -1, jnp.int32).at[a_target].set(a_coord)
    b_send = (
        jnp.zeros((slot_count, edge_size, edge_size), jnp.bfloat16)
        .at[b_target]
        .set(b_blocks[b_source])
    )
    b_where = jnp.full((slot_count, 2), -1, jnp.int32).at[b_target].set(b_coord[b_source])

    def exchange(values, trailing):
        shaped = values.reshape((devices, capacity) + values.shape[1:])
        got = lax.all_to_all(shaped, ("row", "col"), split_axis=0, concat_axis=0, tiled=True)
        return as_slots(got, slot_count, trailing)

    a_recv = exchange(a_send, (edge_size, edge_size))
    b_recv = exchange(b_send, (edge_size, edge_size))
    a_from = exchange(a_where, (2,))
    b_from = exchange(b_where, (2,))
    a_slot_row = jnp.where(a_from[:, 0] >= 0, a_from[:, 0] % block_rows, block_rows)
    a_panel = (
        jnp.zeros((block_rows, edge_size, KB, edge_size), jnp.bfloat16)
        .at[a_slot_row, :, a_from[:, 1] % KB, :]
        .set(a_recv, mode="drop")
    )
    a_matrix = a_panel.reshape(block_rows * edge_size, KB * edge_size)
    b_slot_row = jnp.where(b_from[:, 0] >= 0, b_from[:, 0] % KB, KB)
    b_panel = (
        jnp.zeros((KB, edge_size, block_cols, edge_size), jnp.bfloat16)
        .at[b_slot_row, :, b_from[:, 1] % block_cols, :]
        .set(b_recv, mode="drop")
    )
    b_matrix = b_panel.reshape(KB * edge_size, block_cols * edge_size)
    summed = jnp.zeros((block_rows * edge_size, block_cols * edge_size), jnp.float32)
    for step_index in range(STEPS):
        summed = summed + jnp.dot(a_matrix, b_matrix, preferred_element_type=jnp.float32)
        if step_index + 1 < STEPS:
            a_matrix = from_behind(a_matrix, "col", -1)
            b_matrix = from_behind(b_matrix, "row", -1)
    masked = (
        summed.reshape(block_rows, edge_size, block_cols, edge_size)
        * c_keep.astype(jnp.float32)[:, None, :, None]
    )
    return masked.reshape(block_rows * edge_size, block_cols * edge_size).astype(jnp.bfloat16)


def fused_kernel(
    n_rows, n_cols, cap, rb, cb, bs,
    a_index, b_index, a_send, b_send, keep, out,
    a_parts, b_parts, a_dense, b_dense, acc, stage,
    ax_send, ax_recv, bz_send, bz_recv, bx_send, bx_recv, az_send, az_recv, own_sem, out_sem,
):
    r = lax.axis_index("row")
    z = lax.axis_index("col")
    plane = n_rows * cap
    line = n_cols * cap
    zero_slot = n_rows * n_cols * cap

    barrier = pltpu.get_barrier_semaphore()
    for d in range(1, n_rows):
        pl.semaphore_signal(barrier, inc=1, device_id=(lax.rem(r + d, n_rows), z), device_id_type=MESH)
    for d in range(1, n_cols):
        pl.semaphore_signal(barrier, inc=1, device_id=(r, lax.rem(z + d, n_cols)), device_id_type=MESH)
    pl.semaphore_wait(barrier, n_rows + n_cols - 2)

    def ax(p, d):
        to = lax.rem(r + d, n_rows)
        return pltpu.make_async_remote_copy(
            src_ref=a_send.at[p, to],
            dst_ref=a_parts[p].at[pl.ds(z * plane + r * cap, cap)],
            send_sem=ax_send.at[p, d - 1],
            recv_sem=ax_recv.at[p, d - 1],
            device_id=(to, z),
            device_id_type=MESH,
        )

    def ax_own(p):
        return pltpu.make_async_copy(
            a_send.at[p, r], a_parts[p].at[pl.ds(z * plane + r * cap, cap)], own_sem.at[0, p]
        )

    def bz(p, d):
        to = lax.rem(z + d, n_cols)
        return pltpu.make_async_remote_copy(
            src_ref=b_send.at[p, to],
            dst_ref=b_parts[p].at[pl.ds(r * line + z * cap, cap)],
            send_sem=bz_send.at[p, d - 1],
            recv_sem=bz_recv.at[p, d - 1],
            device_id=(r, to),
            device_id_type=MESH,
        )

    def bz_own(p):
        return pltpu.make_async_copy(
            b_send.at[p, z], b_parts[p].at[pl.ds(r * line + z * cap, cap)], own_sem.at[1, p]
        )

    def bx(p, d):
        section = b_parts[p].at[pl.ds(r * line, line)]
        return pltpu.make_async_remote_copy(
            src_ref=section,
            dst_ref=section,
            send_sem=bx_send.at[p, d - 1],
            recv_sem=bx_recv.at[p, d - 1],
            device_id=(lax.rem(r + d, n_rows), z),
            device_id_type=MESH,
        )

    def az(p, hop, way):
        origin = z - hop * way
        section = a_parts[p].at[pl.ds(origin * plane, plane)]
        return pltpu.make_async_remote_copy(
            src_ref=section,
            dst_ref=section,
            send_sem=az_send.at[p, hop, (way + 1) // 2],
            recv_sem=az_recv.at[p, hop, (way + 1) // 2],
            device_id=(r, z + way),
            device_id_type=MESH,
        )

    def arrived(p, hop, way):
        section = a_parts[p].at[pl.ds((z - hop * way) * plane, plane)]
        return pltpu.make_async_remote_copy(
            src_ref=section,
            dst_ref=section,
            send_sem=az_send.at[p, hop - 1, (way + 1) // 2],
            recv_sem=az_recv.at[p, hop - 1, (way + 1) // 2],
            device_id=(r, z - way),
            device_id_type=MESH,
        )

    def can_send(hop, way):
        if way == 1:
            return jnp.logical_and(z >= hop, z < n_cols - 1)
        return jnp.logical_and(z + hop < n_cols, z > 0)

    def can_receive(hop, way):
        return z >= hop if way == 1 else z + hop < n_cols

    def open_part(p):
        for d in range(1, n_rows):
            ax(p, d).wait_recv()
        ax_own(p).wait()
        for way in (1, -1):
            @pl.when(can_send(0, way))
            def _():
                az(p, 0, way).start()
        for d in range(1, n_cols):
            bz(p, d).wait_recv()
        bz_own(p).wait()
        for d in range(1, n_rows):
            bx(p, d).start()

    def relay(p):
        for hop in range(1, n_cols):
            for way in (1, -1):
                @pl.when(can_receive(hop, way))
                def _():
                    arrived(p, hop, way).wait_recv()
                if hop < n_cols - 1:
                    @pl.when(can_send(hop, way))
                    def _():
                        az(p, hop, way).start()

    def lay_b(p):
        for d in range(1, n_rows):
            bx(p, d).wait_recv()

        def place_b(k, carry):
            rows = pl.ds(pl.multiple_of(k * bs, bs), bs)
            for j in range(cb):
                b_dense[rows, j * bs:(j + 1) * bs] = b_parts[p][b_index[p, k * cb + j]]
            return carry

        lax.fori_loop(0, KB, place_b, 0)

    wide = 2 * bs
    high = rb // 2
    tall = high * bs
    tiles = 2 * (cb * bs // wide)

    def tile_at(t):
        rows = pl.ds(pl.multiple_of((t % 2) * tall, tall), tall)
        cols = pl.ds(pl.multiple_of((t // 2) * wide, wide), wide)
        return rows, cols

    def finish(t):
        rows, cols = tile_at(t)
        return pltpu.make_async_copy(stage.at[rows, cols], out.at[rows, cols], out_sem.at[t])

    def multiply(p):
        def place_a(i, carry):
            rows = pl.ds(pl.multiple_of(i * bs, bs), bs)
            for k in range(KB):
                a_dense[rows, k * bs:(k + 1) * bs] = a_parts[p][a_index[p, i * KB + k]]
            return carry

        lax.fori_loop(0, rb, place_a, 0)

        def tile(t, carry):
            rows, cols = tile_at(t)
            term = jnp.dot(a_dense[rows, :], b_dense[:, cols], preferred_element_type=jnp.float32)
            if p > 0:
                term = acc[rows, cols] + term
            if p + 1 < n_cols:
                acc[rows, cols] = term
                return carry
            for i in range(high):
                top = pl.multiple_of((t % 2) * tall + i * bs, bs)
                kept = keep[pl.ds((t % 2) * high + i, 1), cols]
                stage[pl.ds(top, bs), cols] = (term[i * bs:(i + 1) * bs] * kept).astype(jnp.bfloat16)
            finish(t).start()
            return carry

        lax.fori_loop(0, tiles, tile, 0)

    for p in range(n_cols):
        for d in range(1, n_rows):
            ax(p, d).start()
        ax_own(p).start()
        for d in range(1, n_cols):
            bz(p, d).start()
        bz_own(p).start()
    for p in range(n_cols):
        a_parts[p][zero_slot] = jnp.zeros((bs, bs), jnp.bfloat16)
        b_parts[p][zero_slot] = jnp.zeros((bs, bs), jnp.bfloat16)

    open_part(0)
    for p in range(n_cols):
        if p + 1 < n_cols:
            open_part(p + 1)
        lay_b(p)
        relay(p)
        multiply(p)

    for p in range(n_cols):
        for d in range(1, n_rows):
            ax(p, d).wait_send()
            bx(p, d).wait_send()
        for d in range(1, n_cols):
            bz(p, d).wait_send()
        for hop in range(n_cols - 1):
            for way in (1, -1):
                @pl.when(can_send(hop, way))
                def _():
                    az(p, hop, way).wait_send()

    def settle(t, carry):
        finish(t).wait()
        return carry

    lax.fori_loop(0, tiles, settle, 0)


def slot_sources(owner, count, cap):
    same = owner[:, None] == owner[None, :]
    total = owner.shape[0]
    earlier = jnp.arange(total)[None, :] < jnp.arange(total)[:, None]
    rank = jnp.sum((same & earlier).astype(jnp.int32), axis=1)
    target = owner * cap + rank
    hit = target[:, None] == jnp.arange(count * cap, dtype=jnp.int32)[None, :]
    order = jnp.arange(total, dtype=jnp.int32)[:, None]
    return jnp.max(jnp.where(hit, order, -1), axis=0), hit


def gathered(a_blocks, a_coord, b_blocks, b_coord, c_keep):
    n_rows = lax.axis_size("row")
    n_cols = lax.axis_size("col")
    devices = n_rows * n_cols
    cap = max(2, 128 // devices)
    bs = a_blocks.shape[1]
    rb, cb = c_keep.shape
    a_owner = (a_coord[:, 1] // KB) * n_rows + a_coord[:, 0] // rb
    b_owner = (b_coord[:, 0] // KB) * n_cols + b_coord[:, 1] // cb
    a_source, a_hit = slot_sources(a_owner, devices, cap)
    b_source, b_hit = slot_sources(b_owner, n_cols * n_cols, cap)
    a_place = (a_coord[:, 0] % rb) * KB + a_coord[:, 1] % KB
    b_place = (b_coord[:, 0] % KB) * cb + b_coord[:, 1] % cb
    a_slot = jnp.max(jnp.where(a_hit, a_place[:, None], -1), axis=0)
    b_slot = jnp.max(jnp.where(b_hit, b_place[:, None], -1), axis=0)
    a_send = jnp.take(a_blocks, jnp.maximum(a_source, 0), axis=0, mode="clip")
    b_send = jnp.take(b_blocks, jnp.maximum(b_source, 0), axis=0, mode="clip")
    a_send = a_send.reshape(n_cols, n_rows, cap, bs, bs)
    b_send = b_send.reshape(n_cols, n_cols, cap, bs, bs)

    a_to = a_slot.reshape(n_cols, n_rows, 1, cap).transpose(1, 2, 0, 3)
    b_to = b_slot.reshape(n_cols, 1, n_cols, cap).transpose(1, 2, 0, 3)
    shape = (n_rows, n_cols, n_cols, cap)
    both = jnp.stack([jnp.broadcast_to(a_to, shape), jnp.broadcast_to(b_to, shape)], axis=2)
    both = both.reshape(devices, 2 * n_cols * cap)
    slots = lax.all_to_all(both, ("row", "col"), split_axis=0, concat_axis=0, tiled=True)
    slots = slots.reshape(n_rows, n_cols, 2, n_cols, cap)
    a_mine = slots[:, :, 0].transpose(2, 1, 0, 3).reshape(n_cols, devices * cap)
    b_mine = slots[:, :, 1].transpose(2, 0, 1, 3).reshape(n_cols, devices * cap)

    def invert(mine, places):
        hit = mine[:, :, None] == jnp.arange(places, dtype=jnp.int32)[None, None, :]
        order = jnp.arange(devices * cap, dtype=jnp.int32)[None, :, None]
        return jnp.min(jnp.where(hit, order, devices * cap), axis=1)

    keep = jnp.repeat(c_keep.astype(jnp.float32), bs, axis=1)
    held = devices * cap + 1
    part = pltpu.VMEM((held, bs, bs), jnp.bfloat16)
    dma = pltpu.SemaphoreType.DMA
    return pl.pallas_call(
        functools.partial(fused_kernel, n_rows, n_cols, cap, rb, cb, bs),
        out_shape=jax.ShapeDtypeStruct((rb * bs, cb * bs), jnp.bfloat16),
        in_specs=[
            pl.BlockSpec(memory_space=pltpu.SMEM),
            pl.BlockSpec(memory_space=pltpu.SMEM),
            pl.BlockSpec(memory_space=pl.ANY),
            pl.BlockSpec(memory_space=pl.ANY),
            pl.BlockSpec(memory_space=pltpu.VMEM),
        ],
        out_specs=pl.BlockSpec(memory_space=pl.ANY),
        scratch_shapes=[
            [part] * n_cols,
            [part] * n_cols,
            pltpu.VMEM((rb * bs, KB * bs), jnp.bfloat16),
            pltpu.VMEM((KB * bs, cb * bs), jnp.bfloat16),
            pltpu.VMEM((rb * bs, cb * bs), jnp.float32),
            pltpu.VMEM((rb * bs, cb * bs), jnp.bfloat16),
            dma((n_cols, n_rows - 1)),
            dma((n_cols, n_rows - 1)),
            dma((n_cols, n_cols - 1)),
            dma((n_cols, n_cols - 1)),
            dma((n_cols, n_rows - 1)),
            dma((n_cols, n_rows - 1)),
            dma((n_cols, n_cols - 1, 2)),
            dma((n_cols, n_cols - 1, 2)),
            dma((2, n_cols)),
            dma((2 * (cb // 2),)),
        ],
        compiler_params=pltpu.CompilerParams(
            collective_id=0, has_side_effects=True, vmem_limit_bytes=60 * 2**20
        ),
    )(invert(a_mine, rb * KB), invert(b_mine, KB * cb), a_send, b_send, keep)


def solution(mesh):
    whole_window = mesh.shape["col"] == STEPS
    return jax.shard_map(
        gathered if whole_window else stepwise,
        mesh=mesh,
        in_specs=(
            P(("row", "col"), None, None),
            P(("row", "col"), None),
            P(("row", "col"), None, None),
            P(("row", "col"), None),
            P("row", "col"),
        ),
        out_specs=P("row", "col"),
        check_vma=False,
    )
```
